512 devices in a mesh: dom: 64 (over z, y), rep: 8 (over x, core).
Axes of the slice: x: 4, y: 4, z: 16, core: 2. Of those that a mesh axis runs over, the one named last changes fastest.
Arguments:
- feats: bfloat16 [65536, 128], P(('dom', 'rep')), may hold values from -6 to 6
- weight: bfloat16 [128, 128], replicated, may hold values from -0.5 to 0.5
- bias: float32 [128], replicated, may hold values from -3 to 3
- tiles: bfloat16 [512, 5, 28, 128, 128], P(('dom', 'rep')), may hold values from -0.0625 to 0.0625
- tile_cols: int32 [512, 5, 28], P(('dom', 'rep')), may hold values from 0 to 7
- tile_count: int32 [512, 5], P(('dom', 'rep')), may hold values from 2 to 28, as said below
- cotangent: bfloat16 [65536, 128], P(('dom', 'rep')), may hold values from -6 to 6
Outputs:
- hidden: bfloat16 [65536, 128], P(('dom', 'rep'))
- grad_weight: float32 [128, 128], replicated
- grad_bias: float32 [128], replicated
- grad_feats: bfloat16 [65536, 128], P(('dom', 'rep'))
The draws below stay inside these ranges and needn't reach their ends.
Inputs may be any that keep to these rules, and one draw needn't show every extreme that they name: `tile_count`: every list has at least two live tiles; the nodes of some device have 28 live tiles in every list, and those of most devices far fewer.
All inputs are finite; a program needn't handle non-finite values.
Results may differ from the reference program's by a relative error of at most 0.0062.
Values may be sent and summed in bfloat16 or wider, within the bound.
A program may use at most 64 MiB of HBM per device.

```python
import jax
import jax.numpy as jnp
from jax import lax

F_IN = 128
HID = 128
BLK = 128
TB = 1
MAXT = 28
SLOTS = 5
NODES = 65536
N_DOM = 64
N_REP = 8


def draw_tile_count(key, part):
    first, second, third = jax.random.split(jax.random.fold_in(key, 7), 3)
    block_total = NODES // BLK
    device_total = block_total // TB
    base = jax.random.randint(first, (block_total, SLOTS), 2, MAXT // 2 + 2)
    heavy_device = jax.random.randint(second, (device_total,), 0, 8) == 0
    forced = jax.random.randint(third, (), 0, device_total)
    heavy_device = heavy_device | (jnp.arange(device_total) == forced)
    heavy_block = jnp.repeat(heavy_device, TB)
    return jnp.where(heavy_block[:, None], MAXT, base).astype(jnp.int32)


def place_ends(drawn, stream_key, smallest, largest):
    dims = drawn.shape
    spot = [jax.random.randint(jax.random.fold_in(stream_key, axis), (), 0, dims[axis]) for axis in range(len(dims))]
    drawn = drawn.at[tuple(spot)].set(smallest)
    longest = dims.index(max(dims))
    spot[longest] = (spot[longest] + 1) % dims[longest]
    return drawn.at[tuple(spot)].set(largest)


def shard_levels(stream_key, shape, cuts, least, largest):
    factor_of = 1.0
    for dim, blocks in cuts:
        draws = jax.random.uniform(jax.random.fold_in(jax.random.fold_in(stream_key, 6), dim), (blocks,), jnp.float32, least / len(cuts), largest / len(cuts))
        factor_of = factor_of * jnp.repeat(jnp.exp(draws), shape[dim] // blocks).reshape((-1,) + (1,) * (len(shape) - 1 - dim))
    return factor_of


def normal_values(stream_key, extent, scale, bound, cuts=(), dtype=jnp.bfloat16):
    result = jax.random.normal(stream_key, extent, jnp.float32) * scale
    if len(cuts) > 0:
        result = shard_levels(stream_key, extent, cuts, -0.22, 0.18) * result
    return jnp.clip(result, min=-bound, max=bound).astype(dtype)


def setup_inputs(seed: int = 0) -> dict:
    key_of = jax.random.split(jax.random.key(seed), 8)
    return {
        "feats": normal_values(key_of[0], (NODES, F_IN), 1.0, 6.0, ((0, 512),)),
        "weight": normal_values(key_of[1], (F_IN, HID), F_IN ** -0.5, 0.5),
        "bias": normal_values(key_of[2], (HID,), 0.5, 3.0, (), jnp.float32),
        "tiles": normal_values(key_of[3], (NODES // BLK, SLOTS, MAXT, BLK, BLK), (BLK * MAXT * 2) ** -0.5, 0.0625, ((0, 512),)),
        "tile_cols": place_ends(jax.random.randint(key_of[4], (NODES // BLK, SLOTS, MAXT), 0, N_REP * TB), jax.random.fold_in(key_of[4], 1), 0, (N_REP * TB) - 1).astype(jnp.int32),
        "tile_count": draw_tile_count(jax.random.fold_in(key_of[7], 71), 0),
        "cotangent": normal_values(key_of[6], (NODES, HID), 1.0, 6.0, ((0, 512),)),
    }


def gelu_tanh(values):
    return jax.nn.gelu(values, approximate=True)

def reference(feats, weight, bias, tiles, tile_cols, tile_count, cotangent):
    block_total = NODES // BLK
    panel_blocks = N_REP * TB
    projected = jnp.dot(feats, weight, preferred_element_type=jnp.float32).astype(jnp.bfloat16)
    proj_blocks = projected.reshape(block_total, BLK, HID)
    partition = (jnp.arange(block_total) // panel_blocks).astype(jnp.int32)
    offsets = [0] + [N_DOM >> slot for slot in range(1, SLOTS)]
    source_part = jnp.stack([partition ^ offset for offset in offsets], axis=1).astype(jnp.int32)
    source_block = (source_part[:, :, None] * panel_blocks + tile_cols).astype(jnp.int32)
    live_mask = jnp.arange(MAXT)[None, None, :] < tile_count[:, :, None]

    def forward_block(items):
        tile_set, where_from, keep = items
        fetched = proj_blocks[where_from].astype(jnp.float32)
        fetched = jnp.where(keep[:, :, None, None], fetched, jnp.float32(0.0))
        return jnp.einsum('smij,smjh->ih', tile_set.astype(jnp.float32), fetched)
    summed = lax.map(forward_block, (tiles, source_block, live_mask))
    preact = summed.reshape(NODES, HID) + bias
    hidden_f, pullback = jax.vjp(gelu_tanh, preact)
    hidden = hidden_f.astype(jnp.bfloat16)
    grad_pre = pullback(cotangent.astype(jnp.float32))[0]
    grad_pre_b = grad_pre.astype(jnp.bfloat16).reshape(block_total, BLK, HID)

    def backward_block(carry, items):
        tile_set, where_from, keep, rows = items
        masked = jnp.where(keep[:, :, None, None], tile_set.astype(jnp.float32), jnp.float32(0.0))
        contrib = jnp.einsum('smij,ih->smjh', masked, rows.astype(jnp.float32))
        return (carry.at[where_from].add(contrib), None)
    start = jnp.zeros((block_total, BLK, HID), jnp.float32)
    grad_sum, unused = lax.scan(backward_block, start, (tiles, source_block, live_mask, grad_pre_b))
    grad_proj = grad_sum.reshape(NODES, HID).astype(jnp.bfloat16)
    grad_weight = jnp.dot(feats.T, grad_proj, preferred_element_type=jnp.float32)
    grad_bias = lax.optimization_barrier(jnp.sum(grad_pre, axis=0))
    grad_feats = jnp.dot(grad_proj, weight.T, preferred_element_type=jnp.float32).astype(jnp.bfloat16)
    return (hidden, grad_weight, grad_bias, grad_feats)
```

```python
import jax
import jax.numpy as jnp
from jax import lax
from jax.experimental import pallas as pl
from jax.experimental.pallas import tpu as pltpu
from jax.sharding import PartitionSpec as P

MESH = pl.DeviceIdType.MESH
F32 = jnp.float32
BF16 = jnp.bfloat16
ROWS = 16


def tree_sum(parts):
    while len(parts) > 1:
        parts = [parts[i] + parts[i + 1] for i in range(0, len(parts), 2)]
    return parts[0]


def kernel(
    dom_size, rep_size, y_size,
    feats, weight, bias, tiles, cols, count, cot,
    hidden_o, gw_o, gb_o, gf_o,
    tl, adj, xbuf, pbuf, rbuf, zsend, zrecv, w_v, b_v, cot_v, cols_s, count_s,
    gsend, grecv, asend, arecv, gfull,
    lsem, xs, xr, ps, pr, fzs, fzr, bzs, bzr, gs, gr, as_, ar, ns, nr,
):
    slots, max_tiles, block = tl.shape[0], tl.shape[1], tl.shape[2]
    dom, rep = lax.axis_index("dom"), lax.axis_index("rep")

    def zpeer(k):
        return (jnp.bitwise_xor(dom, dom_size >> k), rep)

    def rpeer(j):
        return (dom, jnp.bitwise_xor(rep, j))

    z_lo = [1 * y_size, 2 * y_size, 3 * y_size]
    z_hi = [4 * y_size, 8 * y_size, 12 * y_size]
    stages = [[1, 2, 3], z_lo, z_hi]
    far = sorted(set(sum(stages, [])) | {dom_size >> k for k in range(1, slots)})

    loc = [
        pltpu.make_async_copy(feats, xbuf.at[0, 0], lsem.at[0]),
        pltpu.make_async_copy(cols.at[0], cols_s, lsem.at[1]),
        pltpu.make_async_copy(count, count_s, lsem.at[2]),
    ]
    order = [0] + list(range(slots - 1, 0, -1))
    tcopy = {k: pltpu.make_async_copy(tiles.at[0, k], tl.at[k], lsem.at[6 + k]) for k in order}
    late = [
        pltpu.make_async_copy(weight, w_v, lsem.at[3]),
        pltpu.make_async_copy(bias, b_v, lsem.at[4]),
        pltpu.make_async_copy(cot, cot_v, lsem.at[5]),
    ]
    for c in loc:
        c.start()
    for k in order:
        tcopy[k].start()
    for c in late:
        c.start()

    barrier = pltpu.get_barrier_semaphore()
    for m in far:
        pl.semaphore_signal(barrier, inc=1, device_id=(jnp.bitwise_xor(dom, m), rep), device_id_type=MESH)
    for j in range(1, rep_size):
        pl.semaphore_signal(barrier, inc=1, device_id=rpeer(j), device_id_type=MESH)

    for c in loc[1:]:
        c.wait()
    chunks = block // ROWS
    width = max_tiles * ROWS
    lane = lax.broadcasted_iota(jnp.int32, (rep_size * ROWS, width), 1)
    row = lax.broadcasted_iota(jnp.int32, (rep_size * ROWS, width), 0)
    diag = (lane & (ROWS - 1)) == (row & (ROWS - 1))
    row_col = row >> (ROWS.bit_length() - 1)
    lane_1 = lax.broadcasted_iota(jnp.int32, (8, width), 1) >> (ROWS.bit_length() - 1)

    def build(k):
        live = count_s[0, k]
        want = jnp.full((8, width), -1, jnp.int32)
        for m in range(max_tiles):
            col = jnp.where(m < live, jnp.bitwise_xor(cols_s[k, m], rep), -1)
            want = jnp.where(lane_1 == m, col, want)
        want = jnp.broadcast_to(want[0:1], (rep_size * ROWS, width))
        sel = jnp.where(diag & (want == row_col), 1.0, 0.0).astype(BF16)
        tcopy[k].wait()
        for c in range(chunks):
            part = tl[k, :, c * ROWS:(c + 1) * ROWS, :].reshape(width, block)
            out = jnp.dot(sel, part, preferred_element_type=F32).astype(BF16)
            for j in range(rep_size):
                adj[k, c * ROWS:(c + 1) * ROWS, j * block:(j + 1) * block] = out[j * ROWS:(j + 1) * ROWS]

    def remote(src, dst, ssem, rsem, peer):
        return pltpu.make_async_remote_copy(
            src_ref=src, dst_ref=dst, send_sem=ssem, recv_sem=rsem, device_id=peer, device_id_type=MESH
        )

    build(order[0])
    build(order[1])
    build(order[2])
    loc[0].wait()
    pl.semaphore_wait(barrier, len(far) + rep_size - 1)

    fz = {}
    for k in range(1, slots):
        fz[k] = remote(xbuf.at[0, 0], xbuf.at[k, 0], fzs.at[k], fzr.at[k], zpeer(k))
        fz[k].start()
    fx = {}

    def spread(k):
        fx[k] = []
        for j in range(1, rep_size):
            c = remote(xbuf.at[k, 0], xbuf.at[k, j], xs.at[k, j], xr.at[k, j], rpeer(j))
            c.start()
            fx[k].append(c)

    def product(k):
        for c in fx[k]:
            c.wait_recv()
        x = xbuf[k].reshape(rep_size * block, block)
        return jnp.dot(adj[k], x, preferred_element_type=F32)

    spread(0)
    for k in order[3:]:
        build(k)
    total = product(0)
    for k in order[1:]:
        fz[k].wait_recv()
        spread(k)
        if k != order[1]:
            total = total + product(k + 1)
    for c in late:
        c.wait()
    total = total + product(order[-1])

    t_hi = total.astype(BF16)
    t_lo = (total - t_hi.astype(F32)).astype(BF16)
    w = w_v[...]
    v = jnp.dot(t_hi, w, preferred_element_type=F32) + jnp.dot(t_lo, w, preferred_element_type=F32) + b_v[...]
    c0 = 0.7978845608028654
    th = jnp.tanh(c0 * (v + 0.044715 * (v * v * v)))
    cdf = 0.5 * (1.0 + th)
    deriv = cdf + 0.5 * v * (1.0 - th * th) * (c0 * (1.0 + 3.0 * 0.044715 * v * v))
    grad_pre = cot_v[...].astype(F32) * deriv
    g = grad_pre.astype(BF16)
    back = lax.dot_general(w, g, (((1,), (1,)), ((), ())), preferred_element_type=F32).astype(BF16)

    bx = {}
    own = {}

    def push(k):
        part = jnp.dot(back, adj[k], preferred_element_type=F32)
        own[k] = part[:, :block]
        bx[k] = []
        for j in range(1, rep_size):
            pbuf[k, j] = part[:, j * block:(j + 1) * block].astype(BF16)
            c = remote(pbuf.at[k, j], rbuf.at[k, j], ps.at[k, j], pr.at[k, j], rpeer(j))
            c.start()
            bx[k].append(c)
        pbuf[k, 0] = own[k].astype(BF16)

    def gathered(k):
        parts = [pbuf[k, 0].astype(F32)]
        for j in range(1, rep_size):
            bx[k][j - 1].wait_recv()
            parts.append(rbuf[k, j].astype(F32))
        return tree_sum(parts)

    push(1)
    gw = lax.dot_general(t_hi, g, (((0,), (0,)), ((), ())), preferred_element_type=F32) + lax.dot_general(
        t_lo, g, (((0,), (0,)), ((), ())), preferred_element_type=F32
    )
    piece = block // rep_size
    gb = jnp.broadcast_to(jnp.sum(grad_pre, axis=0, keepdims=True), (8, block))
    for p in range(rep_size):
        gsend[p, 0:piece, :] = gw[p * piece:(p + 1) * piece]
        gsend[p, piece:, :] = gb
    gx = []
    for j in range(1, rep_size):
        c = remote(gsend.at[jnp.bitwise_xor(rep, j)], grecv.at[j], gs.at[j], gr.at[j], rpeer(j))
        c.start()
        gx.append(c)
    for k in range(2, slots):
        push(k)
    push(0)
    hidden_o[...] = (v * cdf).astype(BF16)

    bz = {}

    def cross(k):
        zsend[k] = gathered(k).astype(BF16)
        bz[k] = remote(zsend.at[k], zrecv.at[k], bzs.at[k], bzr.at[k], zpeer(k))
        bz[k].start()

    ax = []

    def stage(s, value):
        asend[s] = value
        ax.append([])
        for i, m in enumerate(stages[s]):
            c = remote(
                asend.at[s], arecv.at[s, i], as_.at[s, i], ar.at[s, i], (jnp.bitwise_xor(dom, m), rep)
            )
            c.start()
            ax[s].append(c)

    def staged(s):
        for c in ax[s]:
            c.wait_recv()
        return tree_sum([asend[s], arecv[s, 0], arecv[s, 1], arecv[s, 2]])

    cross(1)
    parts = [gsend[rep]]
    for j in range(1, rep_size):
        gx[j - 1].wait_recv()
        parts.append(grecv[j])
    stage(0, tree_sum(parts))
    cross(2)
    stage(1, staged(0))
    cross(3)
    stage(2, staged(1))
    cross(4)
    acc = gathered(0)
    whole = staged(2)
    gfull[rep] = whole[0:piece]
    nx = []
    for j in range(1, rep_size):
        c = remote(gfull.at[rep], gfull.at[rep], ns.at[j], nr.at[j], rpeer(j))
        c.start()
        nx.append(c)
    gb_o[...] = whole[piece:piece + 1]
    for k in range(slots - 1, 0, -1):
        bz[k].wait_recv()
        acc = acc + zrecv[k].astype(F32)
    gf_o[...] = acc.T.astype(BF16)
    for c in nx:
        c.wait_recv()
    gw_o[...] = gfull[...].reshape(block, block)

    for k in range(1, slots):
        fz[k].wait_send()
        bz[k].wait_send()
    for k in range(slots):
        for c in fx[k] + bx[k]:
            c.wait_send()
    for c in gx + nx + ax[0] + ax[1] + ax[2]:
        c.wait_send()


def solution(mesh):
    dom_size, rep_size = mesh.shape["dom"], mesh.shape["rep"]
    y_size = 4

    def body(feats, weight, bias, tiles, tile_cols, tile_count, cot):
        slots, max_tiles, block = tiles.shape[1], tiles.shape[2], tiles.shape[3]
        dma = pltpu.SemaphoreType.DMA
        vmem = pltpu.VMEM
        piece = block // rep_size
        any_spec = pl.BlockSpec(memory_space=pl.ANY)
        out_spec = pl.BlockSpec(memory_space=pltpu.VMEM)
        outs = pl.pallas_call(
            lambda *refs: kernel(dom_size, rep_size, y_size, *refs),
            out_shape=(
                jax.ShapeDtypeStruct((block, block), BF16),
                jax.ShapeDtypeStruct((block, block), F32),
                jax.ShapeDtypeStruct((1, block), F32),
                jax.ShapeDtypeStruct((block, block), BF16),
            ),
            in_specs=[any_spec] * 7,
            out_specs=(out_spec,) * 4,
            scratch_shapes=[
                vmem((slots, max_tiles, block, block), BF16),
                vmem((slots, block, rep_size * block), BF16),
                vmem((slots, rep_size, block, block), BF16),
                vmem((slots, rep_size, block, block), BF16),
                vmem((slots, rep_size, block, block), BF16),
                vmem((slots, block, block), BF16),
                vmem((slots, block, block), BF16),
                vmem((block, block), BF16),
                vmem((1, block), F32),
                vmem((block, block), BF16),
                pltpu.SMEM((slots, max_tiles), jnp.int32),
                pltpu.SMEM((1, slots), jnp.int32),
                vmem((rep_size, piece + 8, block), F32),
                vmem((rep_size, piece + 8, block), F32),
                vmem((3, piece + 8, block), F32),
                vmem((3, 3, piece + 8, block), F32),
                vmem((rep_size, piece, block), F32),
                dma((6 + slots,)),
                dma((slots, rep_size)), dma((slots, rep_size)),
                dma((slots, rep_size)), dma((slots, rep_size)),
                dma((slots,)), dma((slots,)), dma((slots,)), dma((slots,)),
                dma((rep_size,)), dma((rep_size,)),
                dma((3, 3)), dma((3, 3)),
                dma((rep_size,)), dma((rep_size,)),
            ],
            compiler_params=pltpu.CompilerParams(collective_id=0, has_side_effects=True),
            name="gcn_step",
        )(feats, weight, bias.reshape(1, block), tiles, tile_cols, tile_count, cot)
        return outs[0], outs[1], outs[2].reshape(block), outs[3]

    return jax.shard_map(
        body,
        mesh=mesh,
        in_specs=(
            P(("dom", "rep"), None),
            P(),
            P(),
            P(("dom", "rep"), None, None, None, None),
            P(("dom", "rep"), None, None),
            P(("dom", "rep"), None),
            P(("dom", "rep"), None),
        ),
        out_specs=(P(("dom", "rep"), None), P(), P(), P(("dom", "rep"), None)),
        check_vma=False,
    )
```

```python
import jax
import jax.numpy as jnp
from jax import lax
from jax.experimental import pallas as pl
from jax.experimental.pallas import tpu as pltpu
from jax.sharding import PartitionSpec as P

MESH = pl.DeviceIdType.MESH
F32 = jnp.float32
BF16 = jnp.bfloat16
ROWS = 16


def tree_sum(parts):
    while len(parts) > 1:
        parts = [parts[i] + parts[i + 1] for i in range(0, len(parts), 2)]
    return parts[0]


def kernel(
    dom_size, rep_size, y_size,
    feats, weight, bias, tiles, cols, count, cot,
    hidden_o, gw_o, gb_o, gf_o,
    tl, adj, xbuf, pown, psib, qbuf, rsend, rbuf, zsend, zrecv, w_v, b_v, cot_v, cols_s, count_s,
    gsend, grecv, asend, arecv,
    lsem, xs, xr, sibs, sibr, qs, qr, ps, pr, fzs, fzr, bzs, bzr, gs, gr, as_, ar, ns, nr,
):
    slots, max_tiles, block = tl.shape[0], tl.shape[1], tl.shape[2]
    chips = rep_size // 2
    dom, rep = lax.axis_index("dom"), lax.axis_index("rep")
    sibling = (dom, jnp.bitwise_xor(rep, 1))

    def zpeer(k):
        return (jnp.bitwise_xor(dom, dom_size >> k), rep)

    def rpeer(j):
        return (dom, jnp.bitwise_xor(rep, j))

    z_lo = [1 * y_size, 2 * y_size, 3 * y_size]
    z_hi = [4 * y_size, 8 * y_size, 12 * y_size]
    stages = [[1, 2, 3], z_lo, z_hi]
    far = sorted(set(sum(stages, [])) | {dom_size >> k for k in range(1, slots)})

    barrier = pltpu.get_barrier_semaphore()
    for m in far[::-1]:
        pl.semaphore_signal(barrier, inc=1, device_id=(jnp.bitwise_xor(dom, m), rep), device_id_type=MESH)
    for j in range(1, rep_size):
        pl.semaphore_signal(barrier, inc=1, device_id=rpeer(j), device_id_type=MESH)

    loc = [
        pltpu.make_async_copy(feats, xbuf.at[0, 0, 0], lsem.at[0]),
        pltpu.make_async_copy(cols, cols_s, lsem.at[1]),
        pltpu.make_async_copy(count, count_s, lsem.at[2]),
    ]
    order = [0] + list(range(slots - 1, 0, -1))
    tcopy = {k: pltpu.make_async_copy(tiles.at[0, k], tl.at[k], lsem.at[6 + k]) for k in order}
    late = [
        pltpu.make_async_copy(weight, w_v, lsem.at[3]),
        pltpu.make_async_copy(bias, b_v, lsem.at[4]),
        pltpu.make_async_copy(cot, cot_v, lsem.at[5]),
    ]
    for c in loc:
        c.start()
    for k in order:
        tcopy[k].start()
    for c in late:
        c.start()

    def remote(_, src, dst, ssem, rsem, peer):
        return pltpu.make_async_remote_copy(
            src_ref=src, dst_ref=dst, send_sem=ssem, recv_sem=rsem, device_id=peer, device_id_type=MESH
        )

    sent = []

    def go(*args):
        c = remote(*args)
        c.start()
        sent.append(c)
        return c

    chunks = block // ROWS
    width = max_tiles * ROWS
    lane = lax.broadcasted_iota(jnp.int32, (rep_size * ROWS, width), 1)
    row = lax.broadcasted_iota(jnp.int32, (rep_size * ROWS, width), 0)
    diag = (lane & (ROWS - 1)) == (row & (ROWS - 1))
    row_col = row >> (ROWS.bit_length() - 1)
    lane_1 = lax.broadcasted_iota(jnp.int32, (8, width), 1) >> (ROWS.bit_length() - 1)

    def build(k):
        live = count_s[0, k]
        want = jnp.full((8, width), -1, jnp.int32)
        for m in range(max_tiles):
            e = jnp.bitwise_xor(cols_s[k, 0, m], rep)
            col = jnp.where(m < live, (e & 1) * chips + (e >> 1), -1)
            want = jnp.where(lane_1 == m, col, want)
        want = jnp.broadcast_to(want[0:1], (rep_size * ROWS, width))
        sel = jnp.where(diag & (want == row_col), 1.0, 0.0).astype(BF16)
        tcopy[k].wait()
        for c in range(chunks):
            part = tl[k, :, c * ROWS:(c + 1) * ROWS, :].reshape(width, block)
            out = jnp.dot(sel, part, preferred_element_type=F32).astype(BF16)
            for j in range(rep_size):
                adj[k, c * ROWS:(c + 1) * ROWS, j * block:(j + 1) * block] = out[j * ROWS:(j + 1) * ROWS]

    half = chips * block
    fz, fx, fs = {}, {}, {}

    def spread(k):
        fx[k] = [
            go("X", xbuf.at[k, 0, 0], xbuf.at[k, 0, i], xs.at[k, i], xr.at[k, i], rpeer(2 * i)) for i in range(1, chips)
        ]

    def share(k):
        for c in fx[k]:
            c.wait_recv()
        fs[k] = go("X", xbuf.at[k, 0], xbuf.at[k, 1], sibs.at[k], sibr.at[k], sibling)

    def product(k, h):
        if h == 1:
            fs[k].wait_recv()
        return jnp.dot(
            adj[k, :, h * half:(h + 1) * half], xbuf[k, h].reshape(half, block), preferred_element_type=F32
        )

    loc[0].wait()
    pl.semaphore_wait(barrier, len(far) + rep_size - 1)
    for k in range(1, slots):
        fz[k] = go("F", xbuf.at[0, 0, 0], xbuf.at[k, 0, 0], fzs.at[k], fzr.at[k], zpeer(k))
    spread(0)
    for c in loc[1:]:
        c.wait()
    build(0)
    fz[4].wait_recv()
    spread(4)
    fz[3].wait_recv()
    spread(3)
    build(4)
    share(0)
    build(3)
    fz[2].wait_recv()
    spread(2)
    share(4)
    build(2)
    share(3)
    build(1)
    total = product(0, 0) + product(0, 1) + product(4, 0) + product(4, 1)
    share(2)
    fz[1].wait_recv()
    spread(1)
    total = total + product(3, 0) + product(3, 1) + product(2, 0) + product(2, 1)
    for c in late:
        c.wait()
    share(1)
    total = total + product(1, 0)
    total = total + product(1, 1)

    t_hi = total.astype(BF16)
    t_lo = (total - t_hi.astype(F32)).astype(BF16)
    w = w_v[...]
    v = jnp.dot(t_hi, w, preferred_element_type=F32) + jnp.dot(t_lo, w, preferred_element_type=F32) + b_v[...]
    c0 = 0.7978845608028654
    th = jnp.tanh(c0 * (v + 0.044715 * (v * v * v)))
    cdf = 0.5 * (1.0 + th)
    deriv = cdf + 0.5 * v * (1.0 - th * th) * (c0 * (1.0 + 3.0 * 0.044715 * v * v))
    grad_pre = cot_v[...].astype(F32) * deriv
    g = grad_pre.astype(BF16)

    gw = lax.dot_general(t_hi, g, (((0,), (0,)), ((), ())), preferred_element_type=F32) + lax.dot_general(
        t_lo, g, (((0,), (0,)), ((), ())), preferred_element_type=F32
    )
    piece = block // rep_size
    gb = jnp.broadcast_to(jnp.sum(grad_pre, axis=0, keepdims=True), (8, block))
    for p in range(rep_size):
        gsend[p, 0:piece, :] = gw[p * piece:(p + 1) * piece]
        gsend[p, piece:, :] = gb
    gx = [
        go("G", gsend.at[jnp.bitwise_xor(rep, j)], grecv.at[j], gs.at[j], gr.at[j], rpeer(j)) for j in range(1, rep_size)
    ]

    back = lax.dot_general(w, g, (((1,), (1,)), ((), ())), preferred_element_type=F32).astype(BF16)
    bq, bx, bz = {}, {}, {}

    def push(k):
        part = jnp.dot(back, adj[k, :, half:], preferred_element_type=F32)
        for i in range(chips):
            psib[k, i] = part[:, i * block:(i + 1) * block].astype(BF16)
        bq[k] = go("B", psib.at[k], qbuf.at[k], qs.at[k], qr.at[k], sibling)
        part = jnp.dot(back, adj[k, :, :half], preferred_element_type=F32)
        for i in range(chips):
            pown[k, i] = part[:, i * block:(i + 1) * block]

    def pair(k):
        bq[k].wait_recv()
        bx[k] = []
        for i in range(1, chips):
            rsend[k, i] = (pown[k, i] + qbuf[k, i].astype(F32)).astype(BF16)
            bx[k].append(go("B", rsend.at[k, i], rbuf.at[k, i], ps.at[k, i], pr.at[k, i], rpeer(2 * i)))

    def gathered(k):
        part = pown[k, 0] + qbuf[k, 0].astype(F32)
        for i in range(1, chips):
            bx[k][i - 1].wait_recv()
            part = part + rbuf[k, i].astype(F32)
        return part

    def cross(k):
        zsend[k] = gathered(k).astype(BF16)
        bz[k] = go("Z", zsend.at[k], zrecv.at[k], bzs.at[k], bzr.at[k], zpeer(k))

    ax = []

    def stage(s, value):
        asend[s] = value
        ax.append([
            go("G", asend.at[s], arecv.at[s, i], as_.at[s, i], ar.at[s, i], (jnp.bitwise_xor(dom, m), rep))
            for i, m in enumerate(stages[s])
        ])

    def staged(s):
        for c in ax[s]:
            c.wait_recv()
        return tree_sum([asend[s], arecv[s, 0], arecv[s, 1], arecv[s, 2]])

    push(1)
    push(2)
    pair(1)
    push(3)
    parts = [gsend[rep]]
    for j in range(1, rep_size):
        gx[j - 1].wait_recv()
        parts.append(grecv[j])
    stage(0, tree_sum(parts))
    pair(2)
    push(4)
    pair(3)
    push(0)
    cross(1)
    stage(1, staged(0))
    pair(4)
    cross(2)
    pair(0)
    cross(3)
    cross(4)
    stage(2, staged(1))
    acc = gathered(0)
    hidden_o[...] = (v * cdf).astype(BF16)
    for k in range(slots - 1, 1, -1):
        bz[k].wait_recv()
        acc = acc + zrecv[k].astype(F32)
    bz[1].wait_recv()
    gf_o[...] = (acc + zrecv[1].astype(F32)).T.astype(BF16)
    whole = staged(2)
    gw_o[rep] = whole[0:piece]
    nx = [go("G", gw_o.at[rep], gw_o.at[rep], ns.at[j], nr.at[j], rpeer(j)) for j in range(1, rep_size)]
    gb_o[...] = whole[piece:piece + 1]
    for c in nx:
        c.wait_recv()
    for c in sent:
        c.wait_send()


def finish(hidden, gw, gb, gf, hidden_o, gw_o, gb_o, gf_o):
    hidden_o[...] = hidden[...]
    gw_o[...] = gw[...]
    gb_o[...] = gb[...]
    gf_o[...] = gf[...]


def solution(mesh):
    dom_size, rep_size = mesh.shape["dom"], mesh.shape["rep"]
    y_size = 4

    def body(feats, weight, bias, tiles, tile_cols, tile_count, cot):
        slots, max_tiles, block = tiles.shape[1], tiles.shape[2], tiles.shape[3]
        dma = pltpu.SemaphoreType.DMA
        vmem = pltpu.VMEM
        piece = block // rep_size
        chips = rep_size // 2
        any_spec = pl.BlockSpec(memory_space=pl.ANY)
        vmem_spec = pl.BlockSpec(memory_space=pltpu.VMEM)
        outs = pl.pallas_call(
            lambda *refs: kernel(dom_size, rep_size, y_size, *refs),
            out_shape=(
                vmem((block, block), BF16),
                vmem((rep_size, piece, block), F32),
                vmem((1, block), F32),
                vmem((block, block), BF16),
            ),
            in_specs=[any_spec] * 7,
            out_specs=(vmem_spec,) * 4,
            scratch_shapes=[
                vmem((slots, max_tiles, block, block), BF16),
                vmem((slots, block, rep_size * block), BF16),
                vmem((slots, 2, chips, block, block), BF16),
                vmem((slots, chips, block, block), F32),
                vmem((slots, chips, block, block), BF16),
                vmem((slots, chips, block, block), BF16),
                vmem((slots, chips, block, block), BF16),
                vmem((slots, chips, block, block), BF16),
                vmem((slots, block, block), BF16),
                vmem((slots, block, block), BF16),
                vmem((block, block), BF16),
                vmem((1, block), F32),
                vmem((block, block), BF16),
                pltpu.SMEM((slots, 1, max_tiles), jnp.int32),
                pltpu.SMEM((1, slots), jnp.int32),
                vmem((rep_size, piece + 8, block), F32),
                vmem((rep_size, piece + 8, block), F32),
                vmem((3, piece + 8, block), F32),
                vmem((3, 3, piece + 8, block), F32),
                dma((6 + slots,)),
                dma((slots, chips)), dma((slots, chips)),
                dma((slots,)), dma((slots,)), dma((slots,)), dma((slots,)),
                dma((slots, chips)), dma((slots, chips)),
                dma((slots,)), dma((slots,)), dma((slots,)), dma((slots,)),
                dma((rep_size,)), dma((rep_size,)),
                dma((3, 3)), dma((3, 3)),
                dma((rep_size,)), dma((rep_size,)),
            ],
            compiler_params=pltpu.CompilerParams(
                collective_id=0, has_side_effects=True
            ),
            name="gcn_step",
        )(feats, weight, bias.reshape(1, block), tiles, jnp.transpose(tile_cols, (1, 0, 2)), tile_count, cot)
        outs = pl.pallas_call(
            finish,
            out_shape=(
                jax.ShapeDtypeStruct((block, block), BF16),
                jax.ShapeDtypeStruct((block, block), F32),
                jax.ShapeDtypeStruct((1, block), F32),
                jax.ShapeDtypeStruct((block, block), BF16),
            ),
            in_specs=[vmem_spec] * 4,
            out_specs=(vmem_spec,) * 4,
            compiler_params=pltpu.CompilerParams(vmem_limit_bytes=2**20),
            name="finish",
        )(outs[0], outs[1].reshape(block, block), outs[2], outs[3])
        return outs[0], outs[1], outs[2].reshape(block), outs[3]

    return jax.shard_map(
        body,
        mesh=mesh,
        in_specs=(
            P(("dom", "rep"), None),
            P(),
            P(),
            P(("dom", "rep"), None, None, None, None),
            P(("dom", "rep"), None, None),
            P(("dom", "rep"), None),
            P(("dom", "rep"), None),
        ),
        out_specs=(P(("dom", "rep"), None), P(), P(), P(("dom", "rep"), None)),
        check_vma=False,
    )
```

```python
import jax
import jax.numpy as jnp
from jax import lax
from jax.experimental import pallas as pl
from jax.experimental.pallas import tpu as pltpu
from jax.sharding import PartitionSpec as P

MESH = pl.DeviceIdType.MESH
F32 = jnp.float32
BF16 = jnp.bfloat16
ROWS = 16


def tree_sum(parts):
    while len(parts) > 1:
        parts = [parts[i] + parts[i + 1] for i in range(0, len(parts), 2)]
    return parts[0]


def kernel(
    dom_size, rep_size, y_size,
    feats, weight, bias, tiles, cols, count, cot,
    hidden_o, gw_o, gb_o, gf_o,
    tl, adj, xbuf, pown, psib, qbuf, rsend, rbuf, zsend, zrecv, w_v, b_v, cot_v, cols_s, count_s,
    gsend, grecv, asend, arecv, whole_v, full_v,
    lsem, xr, sibr, qr, pr, fzr, bzr, gr, ssem,
):
    slots, max_tiles, block = tl.shape[0], tl.shape[1], tl.shape[2]
    chips = rep_size // 2
    dom, rep = lax.axis_index("dom"), lax.axis_index("rep")
    sibling = (dom, jnp.bitwise_xor(rep, 1))

    def zpeer(k):
        return (jnp.bitwise_xor(dom, dom_size >> k), rep)

    def rpeer(j):
        return (dom, jnp.bitwise_xor(rep, j))

    plane_size = y_size * rep_size
    depth = dom_size // y_size
    plane = jnp.bitwise_and(dom, y_size - 1) * rep_size + rep

    def ppeer(q):
        return (jnp.bitwise_xor(dom, q // rep_size), jnp.bitwise_xor(rep, q % rep_size))

    def dpeer(m):
        return (jnp.bitwise_xor(dom, m * y_size), rep)

    near = [m for m in (depth // 4, 3 * depth // 4, 1, 2, 3)]
    barrier = pltpu.get_barrier_semaphore()
    for m in near:
        pl.semaphore_signal(barrier, inc=1, device_id=dpeer(m), device_id_type=MESH)
    for q in range(plane_size - 1, 0, -1):
        pl.semaphore_signal(barrier, inc=1, device_id=ppeer(q), device_id_type=MESH)

    loc = [
        pltpu.make_async_copy(feats, xbuf.at[0, 0, 0], lsem.at[0]),
        pltpu.make_async_copy(cols, cols_s, lsem.at[1]),
        pltpu.make_async_copy(count, count_s, lsem.at[2]),
    ]
    order = [0] + list(range(slots - 1, 0, -1))
    tcopy = {k: pltpu.make_async_copy(tiles.at[0, k], tl.at[k], lsem.at[6 + k]) for k in order}
    late = [
        pltpu.make_async_copy(weight, w_v, lsem.at[3]),
        pltpu.make_async_copy(bias, b_v, lsem.at[4]),
        pltpu.make_async_copy(cot, cot_v, lsem.at[5]),
    ]
    for c in loc:
        c.start()
    for k in order:
        tcopy[k].start()
    for c in late:
        c.start()

    def remote(_, src, dst, ssem, rsem, peer):
        return pltpu.make_async_remote_copy(
            src_ref=src, dst_ref=dst, send_sem=ssem, recv_sem=rsem, device_id=peer, device_id_type=MESH
        )

    def go(*args):
        c = remote(*args)
        c.start()
        return c

    def arrived(_, ref, sem):
        pltpu.make_async_copy(ref, ref, sem).wait()

    chunks = block // ROWS
    width = max_tiles * ROWS
    lane = lax.broadcasted_iota(jnp.int32, (rep_size * ROWS, width), 1)
    row = lax.broadcasted_iota(jnp.int32, (rep_size * ROWS, width), 0)
    diag = (lane & (ROWS - 1)) == (row & (ROWS - 1))
    row_col = row >> (ROWS.bit_length() - 1)
    lane_1 = lax.broadcasted_iota(jnp.int32, (8, width), 1) >> (ROWS.bit_length() - 1)

    def build(k):
        live = count_s[0, k]
        want = jnp.full((8, width), -1, jnp.int32)
        for m in range(max_tiles):
            e = jnp.bitwise_xor(cols_s[k, 0, m], rep)
            col = jnp.where(m < live, (e & 1) * chips + (e >> 1), -1)
            want = jnp.where(lane_1 == m, col, want)
        want = jnp.broadcast_to(want[0:1], (rep_size * ROWS, width))
        sel = jnp.where(diag & (want == row_col), 1.0, 0.0).astype(BF16)
        tcopy[k].wait()
        for c in range(chunks):
            part = tl[k, :, c * ROWS:(c + 1) * ROWS, :].reshape(width, block)
            out = jnp.dot(sel, part, preferred_element_type=F32).astype(BF16)
            for j in range(rep_size):
                adj[k, c * ROWS:(c + 1) * ROWS, j * block:(j + 1) * block] = out[j * ROWS:(j + 1) * ROWS]

    half = chips * block

    def spread(k):
        for i in range(1, chips):
            go("X", xbuf.at[k, 0, 0], xbuf.at[k, 0, i], ssem.at[1], xr.at[k], rpeer(2 * i))

    def share(k):
        arrived("X", xbuf.at[k, 0, 1:], xr.at[k])
        go("X", xbuf.at[k, 0], xbuf.at[k, 1], ssem.at[2], sibr.at[k], sibling)

    def fetched(k):
        arrived("F", xbuf.at[k, 0, 0], fzr.at[k])

    def product(k, h):
        if h == 1:
            arrived("X", xbuf.at[k, 1], sibr.at[k])
        return jnp.dot(
            adj[k, :, h * half:(h + 1) * half], xbuf[k, h].reshape(half, block), preferred_element_type=F32
        )

    loc[0].wait()
    pl.semaphore_wait(barrier, len(near) + plane_size - 1)
    for k in range(2, slots):
        go("F", xbuf.at[0, 0, 0], xbuf.at[k, 0, 0], ssem.at[0], fzr.at[k], zpeer(k))
    spread(0)
    for c in loc[1:]:
        c.wait()
    build(0)
    fetched(4)
    spread(4)
    fetched(3)
    spread(3)
    share(0)
    build(4)
    fetched(2)
    go("F", xbuf.at[2, 0, 0], xbuf.at[1, 0, 0], ssem.at[0], fzr.at[1], dpeer(3 * depth // 4))
    spread(2)
    build(3)
    share(4)
    share(3)
    build(2)
    build(1)
    total = product(0, 0) + product(0, 1) + product(4, 0) + product(4, 1)
    share(2)
    total = total + product(3, 0) + product(3, 1)
    for c in late:
        c.wait()
    fetched(1)
    spread(1)
    total = total + product(2, 0) + product(2, 1)
    share(1)
    total = total + product(1, 0)
    total = total + product(1, 1)

    t_hi = total.astype(BF16)
    t_lo = (total - t_hi.astype(F32)).astype(BF16)
    w = w_v[...]
    v = jnp.dot(t_hi, w, preferred_element_type=F32) + jnp.dot(t_lo, w, preferred_element_type=F32) + b_v[...]
    c0 = 0.7978845608028654
    th = jnp.tanh(c0 * (v + 0.044715 * (v * v * v)))
    cdf = 0.5 * (1.0 + th)
    deriv = cdf + 0.5 * v * (1.0 - th * th) * (c0 * (1.0 + 3.0 * 0.044715 * v * v))
    grad_pre = cot_v[...].astype(F32) * deriv
    g = grad_pre.astype(BF16)

    gw = lax.dot_general(t_hi, g, (((0,), (0,)), ((), ())), preferred_element_type=F32) + lax.dot_general(
        t_lo, g, (((0,), (0,)), ((), ())), preferred_element_type=F32
    )
    gb = jnp.broadcast_to(jnp.sum(grad_pre, axis=0, keepdims=True), (8, block))
    low = lax.broadcasted_iota(jnp.int32, (8, block), 0) < 4
    for p in range(0, plane_size, 2):
        rows = gw[4 * p:4 * p + 8]
        gsend[p] = jnp.where(low, rows, gb).astype(BF16)
        gsend[p + 1] = jnp.where(low, gb, rows).astype(BF16)
    for q in range(1, plane_size):
        go("G", gsend.at[jnp.bitwise_xor(plane, q)], grecv.at[q], ssem.at[6], gr.at[0], ppeer(q))

    back = lax.dot_general(w, g, (((1,), (1,)), ((), ())), preferred_element_type=F32).astype(BF16)

    def push(k):
        part = jnp.dot(back, adj[k, :, half:], preferred_element_type=F32)
        for i in range(chips):
            psib[k, i] = part[:, i * block:(i + 1) * block].astype(BF16)
        go("B", psib.at[k], qbuf.at[k], ssem.at[3], qr.at[k], sibling)
        part = jnp.dot(back, adj[k, :, :half], preferred_element_type=F32)
        for i in range(chips):
            pown[k, i] = part[:, i * block:(i + 1) * block]

    def pair(k):
        arrived("B", qbuf.at[k], qr.at[k])
        for i in range(1, chips):
            rsend[k, i] = (pown[k, i] + qbuf[k, i].astype(F32)).astype(BF16)
            go("B", rsend.at[k, i], rbuf.at[k, i], ssem.at[4], pr.at[k], rpeer(2 * i))

    def gathered(k):
        arrived("B", rbuf.at[k, 1:], pr.at[k])
        part = pown[k, 0] + qbuf[k, 0].astype(F32)
        for i in range(1, chips):
            part = part + rbuf[k, i].astype(F32)
        return part

    def cross(k):
        zsend[k] = gathered(k).astype(BF16)
        go("Z", zsend.at[k], zrecv.at[k], ssem.at[5], bzr.at[k], zpeer(k))

    push(1)
    push(2)
    pair(1)
    push(3)
    arrived("G", grecv.at[1:], gr.at[0])
    asend[...] = tree_sum([gsend[plane].astype(F32)] + [grecv[q].astype(F32) for q in range(1, plane_size)]).astype(BF16)
    for m in range(1, depth):
        go("G", asend, arecv.at[m], ssem.at[7], gr.at[1], dpeer(m))
    pair(2)
    push(4)
    pair(3)
    push(0)
    cross(1)
    pair(4)
    pair(0)
    cross(2)
    cross(3)
    cross(4)
    acc = gathered(0)
    hidden_o[...] = (v * cdf).astype(BF16)
    arrived("G", arecv.at[1:], gr.at[1])
    whole = tree_sum([asend[...].astype(F32)] + [arecv[m].astype(F32) for m in range(1, depth)])
    whole_v[...] = whole
    full_v[plane] = whole
    for q in range(1, plane_size):
        go("G", whole_v, full_v.at[plane], ssem.at[8], gr.at[2], ppeer(q))
    gb_o[...] = jnp.where((plane & 1) == 0, whole[4:5], whole[0:1])
    for k in range(slots - 1, 0, -1):
        arrived("Z", zrecv.at[k], bzr.at[k])
        acc = acc + zrecv[k].astype(F32)
    gf_o[...] = acc.T.astype(BF16)
    arrived("G", full_v.at[1:], gr.at[2])
    for p in range(0, plane_size, 2):
        gw_o[4 * p:4 * p + 8] = jnp.where(low, full_v[p], full_v[p + 1])
    arrived("F", zsend.at[1:], ssem.at[0])
    arrived("X", rsend.at[:, 1:], ssem.at[1])
    arrived("X", psib, ssem.at[2])
    arrived("B", psib, ssem.at[3])
    arrived("B", rsend.at[:, 1:], ssem.at[4])
    arrived("Z", zsend.at[1:], ssem.at[5])
    arrived("G", grecv.at[1:], ssem.at[6])
    arrived("G", arecv.at[1:], ssem.at[7])
    arrived("G", full_v.at[1:], ssem.at[8])


def finish(hidden, gw, gb, gf, hidden_o, gw_o, gb_o, gf_o):
    hidden_o[...] = hidden[...]
    gw_o[...] = gw[...]
    gb_o[...] = gb[...]
    gf_o[...] = gf[...]


def solution(mesh):
    dom_size, rep_size = mesh.shape["dom"], mesh.shape["rep"]
    y_size = 4

    def body(feats, weight, bias, tiles, tile_cols, tile_count, cot):
        slots, max_tiles, block = tiles.shape[1], tiles.shape[2], tiles.shape[3]
        dma = pltpu.SemaphoreType.DMA
        vmem = pltpu.VMEM
        chips = rep_size // 2
        any_spec = pl.BlockSpec(memory_space=pl.ANY)
        vmem_spec = pl.BlockSpec(memory_space=pltpu.VMEM)
        outs = pl.pallas_call(
            lambda *refs: kernel(dom_size, rep_size, y_size, *refs),
            out_shape=(
                vmem((block, block), BF16),
                vmem((block, block), F32),
                vmem((1, block), F32),
                vmem((block, block), BF16),
            ),
            in_specs=[any_spec] * 7,
            out_specs=(vmem_spec,) * 4,
            scratch_shapes=[
                vmem((slots, max_tiles, block, block), BF16),
                vmem((slots, block, rep_size * block), BF16),
                vmem((slots, 2, chips, block, block), BF16),
                vmem((slots, chips, block, block), F32),
                vmem((slots, chips, block, block), BF16),
                vmem((slots, chips, block, block), BF16),
                vmem((slots, chips, block, block), BF16),
                vmem((slots, chips, block, block), BF16),
                vmem((slots, block, block), BF16),
                vmem((slots, block, block), BF16),
                vmem((block, block), BF16),
                vmem((1, block), F32),
                vmem((block, block), BF16),
                pltpu.SMEM((slots, 1, max_tiles), jnp.int32),
                pltpu.SMEM((1, slots), jnp.int32),
                vmem((y_size * rep_size, 8, block), BF16),
                vmem((y_size * rep_size, 8, block), BF16),
                vmem((8, block), BF16),
                vmem((dom_size // y_size, 8, block), BF16),
                vmem((8, block), F32),
                vmem((y_size * rep_size, 8, block), F32),
                dma((6 + slots,)),
                dma((slots,)), dma((slots,)), dma((slots,)), dma((slots,)), dma((slots,)), dma((slots,)),
                dma((3,)), dma((9,)),
            ],
            compiler_params=pltpu.CompilerParams(
                collective_id=0, has_side_effects=True
            ),
            name="gcn_step",
        )(feats, weight, bias.reshape(1, block), tiles, jnp.transpose(tile_cols, (1, 0, 2)), tile_count, cot)
        outs = pl.pallas_call(
            finish,
            out_shape=(
                jax.ShapeDtypeStruct((block, block), BF16),
                jax.ShapeDtypeStruct((block, block), F32),
                jax.ShapeDtypeStruct((1, block), F32),
                jax.ShapeDtypeStruct((block, block), BF16),
            ),
            in_specs=[vmem_spec] * 4,
            out_specs=(vmem_spec,) * 4,
            compiler_params=pltpu.CompilerParams(vmem_limit_bytes=2**20),
            name="finish",
        )(outs[0], outs[1], outs[2], outs[3])
        return outs[0], outs[1], outs[2].reshape(block), outs[3]

    return jax.shard_map(
        body,
        mesh=mesh,
        in_specs=(
            P(("dom", "rep"), None),
            P(),
            P(),
            P(("dom", "rep"), None, None, None, None),
            P(("dom", "rep"), None, None),
            P(("dom", "rep"), None),
            P(("dom", "rep"), None),
        ),
        out_specs=(P(("dom", "rep"), None), P(), P(), P(("dom", "rep"), None)),
        check_vma=False,
    )
```

```python
import jax
import jax.numpy as jnp
from jax import lax
from jax.experimental import pallas as pl
from jax.experimental.pallas import tpu as pltpu
from jax.sharding import PartitionSpec as P

MESH = pl.DeviceIdType.MESH
F32 = jnp.float32
BF16 = jnp.bfloat16
ROWS = 16


def tree_sum(parts):
    while len(parts) > 1:
        parts = [parts[i] + parts[i + 1] for i in range(0, len(parts), 2)]
    return parts[0]


def kernel(
    dom_size, rep_size, y_size,
    feats, weight, bias, tiles, cols, count, cot,
    hidden_o, gw_o, gb_o, gf_o,
    tl, adj, xbuf, pown, psib, qbuf, rsend, rbuf, zsend, zrecv, w_v, b_v, cot_v, cols_s, count_s,
    gsend, grecv, asend, arecv, whole_v, full_v,
    lsem, xr, sibr, qr, pr, fzr, bzr, half_r, gr, ssem,
):
    slots, max_tiles, block = tl.shape[0], tl.shape[1], tl.shape[2]
    chips = rep_size // 2
    dom, rep = lax.axis_index("dom"), lax.axis_index("rep")
    sibling = (dom, jnp.bitwise_xor(rep, 1))

    def zpeer(k):
        return (jnp.bitwise_xor(dom, dom_size >> k), rep)

    def rpeer(j):
        return (dom, jnp.bitwise_xor(rep, j))

    plane_size = y_size * rep_size
    depth = dom_size // y_size
    plane = jnp.bitwise_and(dom, y_size - 1) * rep_size + rep

    def ppeer(q):
        return (jnp.bitwise_xor(dom, q // rep_size), jnp.bitwise_xor(rep, q % rep_size))

    def dpeer(m):
        return (jnp.bitwise_xor(dom, m * y_size), rep)

    near = [m for m in (depth // 4, 3 * depth // 4, 1, 2, 3)]
    barrier = pltpu.get_barrier_semaphore()
    for m in near:
        pl.semaphore_signal(barrier, inc=1, device_id=dpeer(m), device_id_type=MESH)
    for j in [6, 7, 4, 5, 2, 3, 1]:
        pl.semaphore_signal(barrier, inc=1, device_id=rpeer(j), device_id_type=MESH)
    for q in range(1, y_size):
        pl.semaphore_signal(barrier, inc=1, device_id=ppeer(q * rep_size), device_id_type=MESH)
    wide = sorted(range(1, plane_size), key=lambda q: (-min(q // 8, 4 - q // 8) - min(q % 8 // 2, 4 - q % 8 // 2), -q))
    deep = sorted(range(1, depth), key=lambda m: (-min(m, depth - m), m))

    loc = [
        pltpu.make_async_copy(feats, xbuf.at[0, 0, 0], lsem.at[0]),
        pltpu.make_async_copy(cols, cols_s, lsem.at[1]),
        pltpu.make_async_copy(count, count_s, lsem.at[2]),
    ]
    order = [0] + list(range(slots - 1, 0, -1))
    tcopy = {k: pltpu.make_async_copy(tiles.at[0, k], tl.at[k], lsem.at[6 + k]) for k in order}
    late = [
        pltpu.make_async_copy(weight, w_v, lsem.at[3]),
        pltpu.make_async_copy(bias, b_v, lsem.at[4]),
        pltpu.make_async_copy(cot, cot_v, lsem.at[5]),
    ]
    for c in loc:
        c.start()
    for k in order:
        tcopy[k].start()
    for c in late:
        c.start()

    def remote(_, src, dst, ssem, rsem, peer):
        return pltpu.make_async_remote_copy(
            src_ref=src, dst_ref=dst, send_sem=ssem, recv_sem=rsem, device_id=peer, device_id_type=MESH
        )

    def go(*args):
        c = remote(*args)
        c.start()
        return c

    def arrived(_, ref, sem):
        pltpu.make_async_copy(ref, ref, sem).wait()

    chunks = block // ROWS
    width = max_tiles * ROWS
    lane = lax.broadcasted_iota(jnp.int32, (rep_size * ROWS, width), 1)
    row = lax.broadcasted_iota(jnp.int32, (rep_size * ROWS, width), 0)
    diag = (lane & (ROWS - 1)) == (row & (ROWS - 1))
    row_col = row >> (ROWS.bit_length() - 1)
    lane_1 = lax.broadcasted_iota(jnp.int32, (8, width), 1) >> (ROWS.bit_length() - 1)

    def build(k):
        live = count_s[0, k]
        want = jnp.full((8, width), -1, jnp.int32)
        for m in range(max_tiles):
            e = jnp.bitwise_xor(cols_s[k, 0, m], rep)
            col = jnp.where(m < live, (e & 1) * chips + (e >> 1), -1)
            want = jnp.where(lane_1 == m, col, want)
        want = jnp.broadcast_to(want[0:1], (rep_size * ROWS, width))
        sel = jnp.where(diag & (want == row_col), 1.0, 0.0).astype(BF16)
        tcopy[k].wait()
        for c in range(chunks):
            part = tl[k, :, c * ROWS:(c + 1) * ROWS, :].reshape(width, block)
            out = jnp.dot(sel, part, preferred_element_type=F32).astype(BF16)
            for j in range(rep_size):
                adj[k, c * ROWS:(c + 1) * ROWS, j * block:(j + 1) * block] = out[j * ROWS:(j + 1) * ROWS]

    half = chips * block

    def spread(k, rows=slice(None)):
        for i in (2, 1, 3):
            src = feats if k == 0 else xbuf.at[k, 0, 0, rows]
            go("X", src, xbuf.at[k, 0, i, rows], ssem.at[1], xr.at[k], rpeer(2 * i))

    def share(k):
        arrived("X", xbuf.at[k, 0, 1:], xr.at[k])
        go("X", xbuf.at[k, 0], xbuf.at[k, 1], ssem.at[2], sibr.at[k], sibling)

    def fetched(k):
        arrived("F", xbuf.at[k, 0, 0], fzr.at[k])

    parts = [slice(0, block // 2), slice(block // 2, block)]

    def product(k, h):
        if h == 1:
            arrived("X", xbuf.at[k, 1], sibr.at[k])
        return jnp.dot(
            adj[k, :, h * half:(h + 1) * half], xbuf[k, h].reshape(half, block), preferred_element_type=F32
        )

    pl.semaphore_wait(barrier, len(near) + rep_size + y_size - 2)
    for n, rows in enumerate(parts):
        go("F", feats.at[rows], xbuf.at[2, 0, 0, rows], ssem.at[0], half_r.at[n], zpeer(2))
    for k in range(3, slots):
        go("F", feats, xbuf.at[k, 0, 0], ssem.at[0], fzr.at[k], zpeer(k))
    spread(0)
    for c in loc[1:]:
        c.wait()
    build(0)
    fetched(4)
    spread(4)
    fetched(3)
    spread(3)
    loc[0].wait()
    share(0)
    build(4)
    for n, rows in enumerate(parts):
        arrived("F", xbuf.at[2, 0, 0, rows], half_r.at[n])
        go("F", xbuf.at[2, 0, 0, rows], xbuf.at[1, 0, 0, rows], ssem.at[0], half_r.at[2 + n], dpeer(3 * depth // 4))
    spread(2)
    build(3)
    share(4)
    share(3)
    build(2)
    build(1)
    total = product(0, 0) + product(0, 1) + product(4, 0) + product(4, 1)
    share(2)
    total = total + product(3, 0) + product(3, 1)
    for c in late:
        c.wait()
    for n, rows in enumerate(parts):
        arrived("F", xbuf.at[1, 0, 0, rows], half_r.at[2 + n])
        spread(1, rows)
    total = total + product(2, 0) + product(2, 1)
    share(1)
    total = total + product(1, 0)
    total = total + product(1, 1)

    t_hi = total.astype(BF16)
    t_lo = (total - t_hi.astype(F32)).astype(BF16)
    w = w_v[...]
    v = jnp.dot(t_hi, w, preferred_element_type=F32) + jnp.dot(t_lo, w, preferred_element_type=F32) + b_v[...]
    c0 = 0.7978845608028654
    th = jnp.tanh(c0 * (v + 0.044715 * (v * v * v)))
    cdf = 0.5 * (1.0 + th)
    deriv = cdf + 0.5 * v * (1.0 - th * th) * (c0 * (1.0 + 3.0 * 0.044715 * v * v))
    grad_pre = cot_v[...].astype(F32) * deriv
    g = grad_pre.astype(BF16)

    gw = lax.dot_general(t_hi, g, (((0,), (0,)), ((), ())), preferred_element_type=F32) + lax.dot_general(
        t_lo, g, (((0,), (0,)), ((), ())), preferred_element_type=F32
    )
    gb = jnp.broadcast_to(jnp.sum(grad_pre, axis=0, keepdims=True), (8, block))
    low = lax.broadcasted_iota(jnp.int32, (8, block), 0) < 4
    for p in range(0, plane_size, 2):
        rows = gw[4 * p:4 * p + 8]
        gsend[p] = jnp.where(low, rows, gb).astype(BF16)
        gsend[p + 1] = jnp.where(low, gb, rows).astype(BF16)
    for q in wide:
        go("G", gsend.at[jnp.bitwise_xor(plane, q)], grecv.at[q], ssem.at[6], gr.at[0], ppeer(q))

    back = lax.dot_general(w, g, (((1,), (1,)), ((), ())), preferred_element_type=F32).astype(BF16)

    def push(k):
        part = jnp.dot(back, adj[k, :, half:], preferred_element_type=F32)
        for i in range(chips):
            psib[k, i] = part[:, i * block:(i + 1) * block].astype(BF16)
        go("B", psib.at[k], qbuf.at[k], ssem.at[3], qr.at[k], sibling)
        part = jnp.dot(back, adj[k, :, :half], preferred_element_type=F32)
        for i in range(chips):
            pown[k, i] = part[:, i * block:(i + 1) * block]

    def pair(k):
        arrived("B", qbuf.at[k], qr.at[k])
        for i in range(1, chips):
            rsend[k, i] = (pown[k, i] + qbuf[k, i].astype(F32)).astype(BF16)
            go("B", rsend.at[k, i], rbuf.at[k, i], ssem.at[4], pr.at[k], rpeer(2 * i))

    def gathered(k):
        arrived("B", rbuf.at[k, 1:], pr.at[k])
        part = pown[k, 0] + qbuf[k, 0].astype(F32)
        for i in range(1, chips):
            part = part + rbuf[k, i].astype(F32)
        return part

    def cross(k):
        zsend[k] = gathered(k).astype(BF16)
        go("Z", zsend.at[k], zrecv.at[k], ssem.at[5], bzr.at[k], zpeer(k))

    push(1)
    push(2)
    pair(1)
    push(3)
    arrived("G", grecv.at[1:], gr.at[0])
    asend[...] = tree_sum([gsend[plane].astype(F32)] + [grecv[q].astype(F32) for q in range(1, plane_size)]).astype(BF16)
    for m in deep:
        go("G", asend, arecv.at[m], ssem.at[7], gr.at[1], dpeer(m))
    pair(2)
    push(4)
    pair(3)
    push(0)
    cross(1)
    pair(4)
    pair(0)
    cross(2)
    cross(3)
    cross(4)
    acc = gathered(0)
    hidden_o[...] = (v * cdf).astype(BF16)
    arrived("G", arecv.at[1:], gr.at[1])
    whole = tree_sum([asend[...].astype(F32)] + [arecv[m].astype(F32) for m in range(1, depth)])
    odd = (plane & 1) == 1
    mine = jnp.where(odd, whole[4:8], whole[0:4])
    whole_v[...] = mine
    full_v[plane] = mine
    for q in wide:
        go("G", whole_v, full_v.at[plane], ssem.at[8], gr.at[2], ppeer(q))
    gb_o[...] = jnp.where(odd, whole[0:1], whole[4:5])
    for k in range(slots - 1, 0, -1):
        arrived("Z", zrecv.at[k], bzr.at[k])
        acc = acc + zrecv[k].astype(F32)
    gf_o[...] = acc.T.astype(BF16)
    arrived("G", full_v.at[1:], gr.at[2])
    gw_o[...] = full_v[...].reshape(block, block)
    arrived("F", zsend.at[1:], ssem.at[0])
    arrived("X", rsend.at[:, 1:], ssem.at[1])
    arrived("X", psib, ssem.at[2])
    arrived("B", psib, ssem.at[3])
    arrived("B", rsend.at[:, 1:], ssem.at[4])
    arrived("Z", zsend.at[1:], ssem.at[5])
    arrived("G", grecv.at[1:], ssem.at[6])
    arrived("G", arecv.at[1:], ssem.at[7])
    arrived("G", full_v.at[1:], ssem.at[8])


def finish(hidden, gw, gb, gf, hidden_o, gw_o, gb_o, gf_o):
    hidden_o[...] = hidden[...]
    gw_o[...] = gw[...]
    gb_o[...] = gb[...]
    gf_o[...] = gf[...]


def solution(mesh):
    dom_size, rep_size = mesh.shape["dom"], mesh.shape["rep"]
    y_size = 4

    def body(feats, weight, bias, tiles, tile_cols, tile_count, cot):
        slots, max_tiles, block = tiles.shape[1], tiles.shape[2], tiles.shape[3]
        dma = pltpu.SemaphoreType.DMA
        vmem = pltpu.VMEM
        chips = rep_size // 2
        any_spec = pl.BlockSpec(memory_space=pl.ANY)
        vmem_spec = pl.BlockSpec(memory_space=pltpu.VMEM)
        outs = pl.pallas_call(
            lambda *refs: kernel(dom_size, rep_size, y_size, *refs),
            out_shape=(
                vmem((block, block), BF16),
                vmem((block, block), F32),
                vmem((1, block), F32),
                vmem((block, block), BF16),
            ),
            in_specs=[any_spec] * 7,
            out_specs=(vmem_spec,) * 4,
            scratch_shapes=[
                vmem((slots, max_tiles, block, block), BF16),
                vmem((slots, block, rep_size * block), BF16),
                vmem((slots, 2, chips, block, block), BF16),
                vmem((slots, chips, block, block), F32),
                vmem((slots, chips, block, block), BF16),
                vmem((slots, chips, block, block), BF16),
                vmem((slots, chips, block, block), BF16),
                vmem((slots, chips, block, block), BF16),
                vmem((slots, block, block), BF16),
                vmem((slots, block, block), BF16),
                vmem((block, block), BF16),
                vmem((1, block), F32),
                vmem((block, block), BF16),
                pltpu.SMEM((slots, 1, max_tiles), jnp.int32),
                pltpu.SMEM((1, slots), jnp.int32),
                vmem((y_size * rep_size, 8, block), BF16),
                vmem((y_size * rep_size, 8, block), BF16),
                vmem((8, block), BF16),
                vmem((dom_size // y_size, 8, block), BF16),
                vmem((4, block), F32),
                vmem((y_size * rep_size, 4, block), F32),
                dma((6 + slots,)),
                dma((slots,)), dma((slots,)), dma((slots,)), dma((slots,)), dma((slots,)), dma((slots,)),
                dma((4,)), dma((3,)), dma((9,)),
            ],
            compiler_params=pltpu.CompilerParams(
                collective_id=0, has_side_effects=True
            ),
            name="gcn_step",
        )(feats, weight, bias.reshape(1, block), tiles, jnp.transpose(tile_cols, (1, 0, 2)), tile_count, cot)
        outs = pl.pallas_call(
            finish,
            out_shape=(
                jax.ShapeDtypeStruct((block, block), BF16),
                jax.ShapeDtypeStruct((block, block), F32),
                jax.ShapeDtypeStruct((1, block), F32),
                jax.ShapeDtypeStruct((block, block), BF16),
            ),
            in_specs=[vmem_spec] * 4,
            out_specs=(vmem_spec,) * 4,
            compiler_params=pltpu.CompilerParams(vmem_limit_bytes=2**20),
            name="finish",
        )(outs[0], outs[1], outs[2], outs[3])
        return outs[0], outs[1], outs[2].reshape(block), outs[3]

    return jax.shard_map(
        body,
        mesh=mesh,
        in_specs=(
            P(("dom", "rep"), None),
            P(),
            P(),
            P(("dom", "rep"), None, None, None, None),
            P(("dom", "rep"), None, None),
            P(("dom", "rep"), None),
            P(("dom", "rep"), None),
        ),
        out_specs=(P(("dom", "rep"), None), P(), P(), P(("dom", "rep"), None)),
        check_vma=False,
    )
```

```python
import jax
import jax.numpy as jnp
from jax import lax
from jax.experimental import pallas as pl
from jax.experimental.pallas import tpu as pltpu
from jax.sharding import PartitionSpec as P

MESH = pl.DeviceIdType.MESH
F32 = jnp.float32
BF16 = jnp.bfloat16
ROWS = 16
CUTS = 2


def tree_sum(parts):
    while len(parts) > 1:
        parts = [parts[i] + parts[i + 1] for i in range(0, len(parts), 2)]
    return parts[0]


def kernel(
    dom_size, rep_size, y_size,
    feats, weight, bias, tiles, cols, count, cot,
    hidden_o, gw_o, gb_o, gf_o,
    tl, adj, xbuf, pown, psib, qbuf, rsend, rbuf, zsend, zrecv, w_v, b_v, cot_v, cols_s, count_s,
    gsend, grecv, asend, arecv, whole_v, full_v,
    lsem, xr, sibr, qr, pr, fzr, bzr, half_r, last_r, gr, ssem,
):
    slots, max_tiles, block = tl.shape[0], tl.shape[1], tl.shape[2]
    chips = rep_size // 2
    dom, rep = lax.axis_index("dom"), lax.axis_index("rep")
    sibling = (dom, jnp.bitwise_xor(rep, 1))

    def zpeer(k):
        return (jnp.bitwise_xor(dom, dom_size >> k), rep)

    def rpeer(j):
        return (dom, jnp.bitwise_xor(rep, j))

    plane_size = y_size * rep_size
    depth = dom_size // y_size
    plane = jnp.bitwise_and(dom, y_size - 1) * rep_size + rep

    def ppeer(q):
        return (jnp.bitwise_xor(dom, q // rep_size), jnp.bitwise_xor(rep, q % rep_size))

    def dpeer(m):
        return (jnp.bitwise_xor(dom, m * y_size), rep)

    near = [m for m in (depth // 4, 3 * depth // 4, 1, 2, 3)]
    barrier = pltpu.get_barrier_semaphore()
    for m in near:
        pl.semaphore_signal(barrier, inc=1, device_id=dpeer(m), device_id_type=MESH)
    for j in [6, 7, 4, 5, 2, 3, 1]:
        pl.semaphore_signal(barrier, inc=1, device_id=rpeer(j), device_id_type=MESH)
    for q in range(1, y_size):
        pl.semaphore_signal(barrier, inc=1, device_id=ppeer(q * rep_size), device_id_type=MESH)
    wide = sorted(range(1, plane_size), key=lambda q: (-min(q // 8, 4 - q // 8) - min(q % 8 // 2, 4 - q % 8 // 2), -q))
    deep = sorted(range(1, depth), key=lambda m: (-min(m, depth - m), m))

    loc = [
        pltpu.make_async_copy(feats, xbuf.at[0, 0, 0], lsem.at[0]),
        pltpu.make_async_copy(cols, cols_s, lsem.at[1]),
        pltpu.make_async_copy(count, count_s, lsem.at[2]),
    ]
    order = [0] + list(range(slots - 1, 0, -1))
    tcopy = {k: pltpu.make_async_copy(tiles.at[0, k], tl.at[k], lsem.at[6 + k]) for k in order}
    late = [
        pltpu.make_async_copy(weight, w_v, lsem.at[3]),
        pltpu.make_async_copy(bias, b_v, lsem.at[4]),
        pltpu.make_async_copy(cot, cot_v, lsem.at[5]),
    ]
    for c in loc:
        c.start()
    for k in order:
        tcopy[k].start()
    for c in late:
        c.start()

    def remote(_, src, dst, ssem, rsem, peer):
        return pltpu.make_async_remote_copy(
            src_ref=src, dst_ref=dst, send_sem=ssem, recv_sem=rsem, device_id=peer, device_id_type=MESH
        )

    def go(*args):
        c = remote(*args)
        c.start()
        return c

    def arrived(_, ref, sem):
        pltpu.make_async_copy(ref, ref, sem).wait()

    chunks = block // ROWS
    width = max_tiles * ROWS
    lane = lax.broadcasted_iota(jnp.int32, (rep_size * ROWS, width), 1)
    row = lax.broadcasted_iota(jnp.int32, (rep_size * ROWS, width), 0)
    diag = (lane & (ROWS - 1)) == (row & (ROWS - 1))
    row_col = row >> (ROWS.bit_length() - 1)
    lane_1 = lax.broadcasted_iota(jnp.int32, (8, width), 1) >> (ROWS.bit_length() - 1)

    def build(k):
        live = count_s[0, k]
        want = jnp.full((8, width), -1, jnp.int32)
        for m in range(max_tiles):
            e = jnp.bitwise_xor(cols_s[k, 0, m], rep)
            col = jnp.where(m < live, (e & 1) * chips + (e >> 1), -1)
            want = jnp.where(lane_1 == m, col, want)
        want = jnp.broadcast_to(want[0:1], (rep_size * ROWS, width))
        sel = jnp.where(diag & (want == row_col), 1.0, 0.0).astype(BF16)
        tcopy[k].wait()
        for c in range(chunks):
            part = tl[k, :, c * ROWS:(c + 1) * ROWS, :].reshape(width, block)
            out = jnp.dot(sel, part, preferred_element_type=F32).astype(BF16)
            for j in range(rep_size):
                adj[k, c * ROWS:(c + 1) * ROWS, j * block:(j + 1) * block] = out[j * ROWS:(j + 1) * ROWS]

    half = chips * block

    def spread(k, rows=slice(None), sem=None):
        for i in (2, 1, 3):
            src = feats if k == 0 else xbuf.at[k, 0, 0, rows]
            go("X", src, xbuf.at[k, 0, i, rows], ssem.at[1], xr.at[k] if sem is None else sem, rpeer(2 * i))

    def share(k):
        arrived("X", xbuf.at[k, 0, 1:], xr.at[k])
        go("X", xbuf.at[k, 0], xbuf.at[k, 1], ssem.at[2], sibr.at[k], sibling)

    def fetched(k):
        arrived("F", xbuf.at[k, 0, 0], fzr.at[k])

    step = block // CUTS
    parts = [slice(n * step, (n + 1) * step) for n in range(CUTS)]

    def product(k, h):
        if h == 1:
            arrived("X", xbuf.at[k, 1], sibr.at[k])
        return jnp.dot(
            adj[k, :, h * half:(h + 1) * half], xbuf[k, h].reshape(half, block), preferred_element_type=F32
        )

    pl.semaphore_wait(barrier, len(near) + rep_size + y_size - 2)
    for n, rows in enumerate(parts):
        go("F", feats.at[rows], xbuf.at[2, 0, 0, rows], ssem.at[0], half_r.at[n], zpeer(2))
    for k in range(3, slots):
        go("F", feats, xbuf.at[k, 0, 0], ssem.at[0], fzr.at[k], zpeer(k))
    spread(0)
    for c in loc[1:]:
        c.wait()
    build(0)
    fetched(4)
    spread(4)
    fetched(3)
    spread(3)
    loc[0].wait()
    share(0)
    build(4)
    for n, rows in enumerate(parts):
        arrived("F", xbuf.at[2, 0, 0, rows], half_r.at[n])
        go("F", xbuf.at[2, 0, 0, rows], xbuf.at[1, 0, 0, rows], ssem.at[0], half_r.at[CUTS + n], dpeer(3 * depth // 4))
    spread(2)
    build(3)
    share(4)
    share(3)
    build(2)
    build(1)
    total = product(0, 0) + product(0, 1) + product(4, 0) + product(4, 1)
    share(2)
    total = total + product(3, 0) + product(3, 1)
    for c in late:
        c.wait()
    for n, rows in enumerate(parts):
        arrived("F", xbuf.at[1, 0, 0, rows], half_r.at[CUTS + n])
        spread(1, rows, last_r.at[2 * n // CUTS])
    total = total + product(2, 0) + product(2, 1)
    for n, rows in enumerate((slice(0, block // 2), slice(block // 2, block))):
        arrived("X", xbuf.at[1, 0, 1:, rows], last_r.at[n])
        go("X", xbuf.at[1, 0, :, rows], xbuf.at[1, 1, :, rows], ssem.at[2], sibr.at[1], sibling)
    total = total + product(1, 0)
    total = total + product(1, 1)

    t_hi = total.astype(BF16)
    t_lo = (total - t_hi.astype(F32)).astype(BF16)
    w = w_v[...]
    v = jnp.dot(
        jnp.concatenate([t_hi, t_lo], axis=1), jnp.concatenate([w, w], axis=0), preferred_element_type=F32
    ) + b_v[...]
    c0 = 0.7978845608028654
    th = jnp.tanh(c0 * (v + 0.044715 * (v * v * v)))
    cdf = 0.5 * (1.0 + th)
    deriv = cdf + 0.5 * v * (1.0 - th * th) * (c0 * (1.0 + 3.0 * 0.044715 * v * v))
    grad_pre = cot_v[...].astype(F32) * deriv
    g = grad_pre.astype(BF16)

    gw = lax.dot_general(
        jnp.concatenate([t_hi, t_lo], axis=0),
        jnp.concatenate([g, g], axis=0),
        (((0,), (0,)), ((), ())),
        preferred_element_type=F32,
    )
    gb = jnp.broadcast_to(jnp.sum(grad_pre, axis=0, keepdims=True), (8, block))
    low = lax.broadcasted_iota(jnp.int32, (8, block), 0) < 4
    for p in range(0, plane_size, 2):
        rows = gw[4 * p:4 * p + 8]
        gsend[p] = jnp.where(low, rows, gb).astype(BF16)
        gsend[p + 1] = jnp.where(low, gb, rows).astype(BF16)
    for q in wide:
        go("G", gsend.at[jnp.bitwise_xor(plane, q)], grecv.at[q], ssem.at[6], gr.at[0], ppeer(q))

    back = lax.dot_general(w, g, (((1,), (1,)), ((), ())), preferred_element_type=F32).astype(BF16)

    def push(k):
        part = jnp.dot(back, adj[k, :, half:], preferred_element_type=F32)
        for i in range(chips):
            psib[k, i] = part[:, i * block:(i + 1) * block].astype(BF16)
        go("B", psib.at[k], qbuf.at[k], ssem.at[3], qr.at[k], sibling)
        part = jnp.dot(back, adj[k, :, :half], preferred_element_type=F32)
        for i in range(chips):
            pown[k, i] = part[:, i * block:(i + 1) * block]

    def pair(k):
        arrived("B", qbuf.at[k], qr.at[k])
        for i in range(1, chips):
            rsend[k, i] = (pown[k, i] + qbuf[k, i].astype(F32)).astype(BF16)
            go("B", rsend.at[k, i], rbuf.at[k, i], ssem.at[4], pr.at[k], rpeer(2 * i))

    def gathered(k):
        arrived("B", rbuf.at[k, 1:], pr.at[k])
        part = pown[k, 0] + qbuf[k, 0].astype(F32)
        for i in range(1, chips):
            part = part + rbuf[k, i].astype(F32)
        return part

    def cross(k):
        zsend[k] = gathered(k).astype(BF16)
        go("Z", zsend.at[k], zrecv.at[k], ssem.at[5], bzr.at[k], zpeer(k))

    push(1)
    push(2)
    pair(1)
    push(3)
    arrived("G", grecv.at[1:], gr.at[0])
    asend[...] = tree_sum([gsend[plane].astype(F32)] + [grecv[q].astype(F32) for q in range(1, plane_size)]).astype(BF16)
    for m in deep:
        go("G", asend, arecv.at[m], ssem.at[7], gr.at[1], dpeer(m))
    pair(2)
    push(4)
    pair(3)
    push(0)
    cross(1)
    pair(4)
    pair(0)
    cross(2)
    cross(3)
    arrived("G", arecv.at[1:], gr.at[1])
    whole = tree_sum([asend[...].astype(F32)] + [arecv[m].astype(F32) for m in range(1, depth)])
    odd = (plane & 1) == 1
    mine = jnp.where(odd, whole[4:8], whole[0:4])
    whole_v[...] = mine
    full_v[plane] = mine
    for q in wide:
        go("G", whole_v, full_v.at[plane], ssem.at[8], gr.at[2], ppeer(q))
    gb_o[...] = jnp.where(odd, whole[0:1], whole[4:5])
    cross(4)
    acc = gathered(0)
    hidden_o[...] = (v * cdf).astype(BF16)
    for k in range(slots - 1, 0, -1):
        arrived("Z", zrecv.at[k], bzr.at[k])
        acc = acc + zrecv[k].astype(F32)
    gf_o[...] = acc.T.astype(BF16)
    arrived("G", full_v.at[1:], gr.at[2])
    gw_o[...] = full_v[...].reshape(block, block)
    arrived("F", zsend.at[1:], ssem.at[0])
    arrived("X", rsend.at[:, 1:], ssem.at[1])
    arrived("X", psib, ssem.at[2])
    arrived("B", psib, ssem.at[3])
    arrived("B", rsend.at[:, 1:], ssem.at[4])
    arrived("Z", zsend.at[1:], ssem.at[5])
    arrived("G", grecv.at[1:], ssem.at[6])
    arrived("G", arecv.at[1:], ssem.at[7])
    arrived("G", full_v.at[1:], ssem.at[8])


def finish(hidden, gw, gb, gf, hidden_o, gw_o, gb_o, gf_o):
    hidden_o[...] = hidden[...]
    gw_o[...] = gw[...]
    gb_o[...] = gb[...]
    gf_o[...] = gf[...]


def solution(mesh):
    dom_size, rep_size = mesh.shape["dom"], mesh.shape["rep"]
    y_size = 4

    def body(feats, weight, bias, tiles, tile_cols, tile_count, cot):
        slots, max_tiles, block = tiles.shape[1], tiles.shape[2], tiles.shape[3]
        dma = pltpu.SemaphoreType.DMA
        vmem = pltpu.VMEM
        chips = rep_size // 2
        any_spec = pl.BlockSpec(memory_space=pl.ANY)
        vmem_spec = pl.BlockSpec(memory_space=pltpu.VMEM)
        outs = pl.pallas_call(
            lambda *refs: kernel(dom_size, rep_size, y_size, *refs),
            out_shape=(
                vmem((block, block), BF16),
                vmem((block, block), F32),
                vmem((1, block), F32),
                vmem((block, block), BF16),
            ),
            in_specs=[any_spec] * 7,
            out_specs=(vmem_spec,) * 4,
            scratch_shapes=[
                vmem((slots, max_tiles, block, block), BF16),
                vmem((slots, block, rep_size * block), BF16),
                vmem((slots, 2, chips, block, block), BF16),
                vmem((slots, chips, block, block), F32),
                vmem((slots, chips, block, block), BF16),
                vmem((slots, chips, block, block), BF16),
                vmem((slots, chips, block, block), BF16),
                vmem((slots, chips, block, block), BF16),
                vmem((slots, block, block), BF16),
                vmem((slots, block, block), BF16),
                vmem((block, block), BF16),
                vmem((1, block), F32),
                vmem((block, block), BF16),
                pltpu.SMEM((slots, 1, max_tiles), jnp.int32),
                pltpu.SMEM((1, slots), jnp.int32),
                vmem((y_size * rep_size, 8, block), BF16),
                vmem((y_size * rep_size, 8, block), BF16),
                vmem((8, block), BF16),
                vmem((dom_size // y_size, 8, block), BF16),
                vmem((4, block), F32),
                vmem((y_size * rep_size, 4, block), F32),
                dma((6 + slots,)),
                dma((slots,)), dma((slots,)), dma((slots,)), dma((slots,)), dma((slots,)), dma((slots,)),
                dma((2 * CUTS,)), dma((2,)), dma((3,)), dma((9,)),
            ],
            compiler_params=pltpu.CompilerParams(
                collective_id=0, has_side_effects=True
            ),
            name="gcn_step",
        )(feats, weight, bias.reshape(1, block), tiles, jnp.transpose(tile_cols, (1, 0, 2)), tile_count, cot)
        outs = pl.pallas_call(
            finish,
            out_shape=(
                jax.ShapeDtypeStruct((block, block), BF16),
                jax.ShapeDtypeStruct((block, block), F32),
                jax.ShapeDtypeStruct((1, block), F32),
                jax.ShapeDtypeStruct((block, block), BF16),
            ),
            in_specs=[vmem_spec] * 4,
            out_specs=(vmem_spec,) * 4,
            compiler_params=pltpu.CompilerParams(vmem_limit_bytes=2**20),
            name="finish",
        )(outs[0], outs[1], outs[2], outs[3])
        return outs[0], outs[1], outs[2].reshape(block), outs[3]

    return jax.shard_map(
        body,
        mesh=mesh,
        in_specs=(
            P(("dom", "rep"), None),
            P(),
            P(),
            P(("dom", "rep"), None, None, None, None),
            P(("dom", "rep"), None, None),
            P(("dom", "rep"), None),
            P(("dom", "rep"), None),
        ),
        out_specs=(P(("dom", "rep"), None), P(), P(), P(("dom", "rep"), None)),
        check_vma=False,
    )
```
